32 devices in a mesh: groups: 2 (over y), wide: 4 (over z), expert: 2 (over x), inner: 2 (over core).
Axes of the slice: x: 2, y: 2, z: 4, core: 2. Of those that a mesh axis runs over, the one named last changes fastest.
Arguments:
- candidates: bfloat16 [4096, 1024], P(('groups', 'wide')), parts along dimension 0, may hold values from -6 to 6
- gate_weight: bfloat16 [1024, 128], replicated
- expert_in: bfloat16 [32, 1024, 2048], P('expert', None, ('wide', 'inner')), may hold values from -0.1875 to 0.1875
- expert_out: bfloat16 [32, 256, 2048], P('expert', None, ('wide', 'inner')), may hold values from -0.125 to 0.125
- norm_gain: bfloat16 [1024], replicated, may hold values from 0.099609375 to 1.8984375
- query_weight: bfloat16 [1024, 1024], P(None, ('expert', 'inner'))
- key_weight: bfloat16 [1024, 1024], P(None, ('expert', 'inner'))
- value_weight: bfloat16 [1024, 1024], P(None, ('expert', 'inner')), may hold values from -0.1875 to 0.1875
- task_weight: bfloat16 [1024, 4], replicated, may hold values from -0.1875 to 0.1875
- attn_weight: bfloat16 [1024, 4], P(('expert', 'inner')), may hold values from -0.75 to 0.75
- request_of: int32 [4096], P(('groups', 'wide')), parts along dimension 0, may hold values from 0 to 7, as said below
Outputs:
- scores: float32 [4096, 4], P(('groups', 'wide')), parts along dimension 0
The draws below stay inside these ranges and needn't reach their ends.
There are 2 independent parts, one for each index of `groups`. The reference program is written for one: setup_inputs(seed, part) draws one part's arguments, and reference() takes and returns one part's arrays. A program takes and returns all parts, laid end to end along the dimension named above; an argument that names none is the same for every part. Nothing has to cross between parts.
Inputs may be any that keep to these rules, and one draw needn't show every extreme that they name: `request_of`: candidates of a request arrive in any order over the shards. Among the 512 candidates of one shard of wide, no request has more than 128; one request has exactly 128 in every shard.
All inputs are finite; a program needn't handle non-finite values.
Results may differ from the reference program's by a relative error of at most 0.0051.
Values may be sent and summed in bfloat16 or wider, within the bound.
A program may use at most 128 MiB of HBM per device.

```python
import math
import jax
import jax.numpy as jnp
from jax import lax

D = 1024
EXPERTS = 32
FF = 2048
DE = 256
TASKS = 4
HEADS = 16
HD = 64
ROW_DEV = 512
ROWS = 2048
REQUEST_TOTAL = 8
CAP = 128
MODEL = 1024
N_WIDE = 4


def draw_gate_weight(key, part):
    first = jax.random.fold_in(key, 0)
    base = jax.random.normal(first, (D, TASKS * EXPERTS), jnp.float32) * D ** (-0.5)
    factors = jnp.full((1, TASKS * EXPERTS), 3.0, jnp.float32)
    return (base * factors).astype(jnp.bfloat16)


def paired_parts(key):
    shared = jax.random.fold_in(key, 7)
    first, second = jax.random.split(shared, 2)
    key_part = jax.random.normal(first, (MODEL, HEADS * HD), jnp.float32) * MODEL ** (-0.5)
    jitter_sample = jax.random.normal(second, (MODEL, HEADS * HD), jnp.float32) * MODEL ** (-0.5)
    return (key_part, jitter_sample)


def draw_query_weight(key, part):
    key_part, jitter_sample = paired_parts(key)
    result = jitter_sample
    return result.astype(jnp.bfloat16)


def draw_key_weight(key, part):
    key_part, jitter_sample = paired_parts(key)
    return key_part.astype(jnp.bfloat16)


def draw_request_of(key, part):
    first, second, third, fourth = jax.random.split(key, 4)
    blocks = ROWS // ROW_DEV
    place_entries = REQUEST_TOTAL * CAP
    tier_value = jax.random.randint(first, (REQUEST_TOTAL,), 0, 4)
    selected_experts = jax.random.randint(second, (), 0, REQUEST_TOTAL)
    extra_credit = jnp.where(jnp.arange(REQUEST_TOTAL) == selected_experts, 131072, tier_value * 16384)
    request_per_place = jnp.arange(place_entries, dtype=jnp.int32) // CAP
    jitter_sample = jax.random.randint(third, (blocks, place_entries), 0, 65536)
    ranking_weight = (extra_credit[request_per_place][None, :] + jitter_sample) * place_entries + jnp.arange(place_entries, dtype=jnp.int32)[None, :]
    picked = lax.top_k(ranking_weight.astype(jnp.int32), ROW_DEV)[1]
    requests = request_per_place[picked]
    shuffles = jax.vmap(lambda sub: jax.random.permutation(sub, ROW_DEV))(jax.random.split(fourth, blocks))
    mixed = jnp.take_along_axis(requests, shuffles, axis=1)
    return mixed.reshape(-1).astype(jnp.int32)


def steps_of(stream_key, dims, cuts, low, top_value):
    def one(dim, parts):
        steps = jax.random.uniform(jax.random.fold_in(jax.random.fold_in(stream_key, 6), dim), (parts,), jnp.float32, low / len(cuts), top_value / len(cuts))
        return jnp.repeat(jnp.exp(steps), dims[dim] // parts).reshape((-1,) + (1,) * (len(dims) - dim - 1))

    level = one(*cuts[0])
    for cut in cuts[1:]:
        level = level * one(*cut)
    return level


def gaussian(own_key, shape, width, limit, pieces=(), held_as=jnp.bfloat16):
    values = width * jax.random.normal(own_key, shape, jnp.float32)
    if pieces:
        values = values * steps_of(own_key, shape, pieces, -0.22, 0.18)
    return jnp.clip(values, -limit, limit).astype(held_as)


def setup_inputs(seed: int = 0, part: int = 0) -> dict:
    arg_keys = jax.random.split(jax.random.key(seed), 12)
    part_keys = jax.random.split(jax.random.fold_in(arg_keys[11], part), 12)
    return {
        "candidates": gaussian(part_keys[0], (ROWS, D), 1.0, 6.0, ((0, 4),)),
        "gate_weight": draw_gate_weight(jax.random.fold_in(arg_keys[11], 71), part),
        "expert_in": gaussian(arg_keys[2], (EXPERTS, D, FF), D ** -0.5, 0.1875, ((0, 2), (2, 8))),
        "expert_out": gaussian(arg_keys[3], (EXPERTS, DE, FF), FF ** -0.5, 0.125, ((0, 2), (2, 8))),
        "norm_gain": jnp.clip(1.0 + 0.18 * jax.random.normal(arg_keys[4], (MODEL,), jnp.float32), 0.099609375, 1.8984375).astype(jnp.bfloat16),
        "query_weight": draw_query_weight(jax.random.fold_in(arg_keys[11], 71), part),
        "key_weight": draw_key_weight(jax.random.fold_in(arg_keys[11], 71), part),
        "value_weight": gaussian(arg_keys[7], (MODEL, HEADS * HD), MODEL ** -0.5, 0.1875, ((1, 4),)),
        "task_weight": gaussian(arg_keys[8], (MODEL, TASKS), MODEL ** -0.5, 0.1875),
        "attn_weight": gaussian(arg_keys[9], (HEADS * HD, TASKS), (HEADS * HD // 16) ** -0.5, 0.75, ((0, 4),)),
        "request_of": draw_request_of(jax.random.fold_in(jax.random.fold_in(arg_keys[11], part), 71), part),
    }


def reference(candidates, gate_weight, expert_in, expert_out, norm_gain, query_weight, key_weight, value_weight, task_weight, attn_weight, request_of):
    logits = jnp.dot(candidates, gate_weight, preferred_element_type=jnp.float32).reshape(ROWS, TASKS, EXPERTS)
    gates = jax.nn.softmax(logits, axis=-1)

    def one_expert(total, index):
        w_in = expert_in[index]
        w_out = expert_out[index]
        hidden = jax.nn.relu(jnp.dot(candidates, w_in, preferred_element_type=jnp.float32)).astype(jnp.bfloat16)
        output = jnp.dot(hidden, w_out.T, preferred_element_type=jnp.float32)
        weight = lax.dynamic_index_in_dim(gates, index, 2, keepdims=False)
        return (total + weight[:, :, None] * output[:, None, :], None)
    mixed, _ = lax.scan(one_expert, jnp.zeros((ROWS, TASKS, DE), jnp.float32), jnp.arange(EXPERTS, dtype=jnp.int32))
    rep = mixed.reshape(ROWS, MODEL)
    center = lax.optimization_barrier(jnp.mean(rep, axis=1, keepdims=True))
    spread = lax.optimization_barrier(jnp.mean(jnp.square(rep - center), axis=1, keepdims=True))
    normed = ((rep - center) * lax.rsqrt(spread + 1e-05) * norm_gain.astype(jnp.float32)).astype(jnp.bfloat16)
    queries = jnp.dot(normed, query_weight, preferred_element_type=jnp.float32).astype(jnp.bfloat16)
    keys = jnp.dot(normed, key_weight, preferred_element_type=jnp.float32).astype(jnp.bfloat16)
    values = jnp.dot(normed, value_weight, preferred_element_type=jnp.float32).astype(jnp.bfloat16)
    order = jnp.argsort(request_of, stable=True).astype(jnp.int32)
    counts = lax.optimization_barrier(jnp.sum((request_of[None, :] == jnp.arange(REQUEST_TOTAL, dtype=jnp.int32)[:, None]).astype(jnp.int32), axis=1))
    offsets = (jnp.cumsum(counts) - counts).astype(jnp.int32)
    span = N_WIDE * CAP
    position = jnp.arange(span, dtype=jnp.int32)
    factor = 1.0 / math.sqrt(HD)

    def one_request(index):
        rows_at = jnp.take(order, jnp.minimum(offsets[index] + position, ROWS - 1).astype(jnp.int32))
        live = position < counts[index]
        query = jnp.take(queries, rows_at, axis=0).astype(jnp.float32).reshape(span, HEADS, HD)
        key = jnp.take(keys, rows_at, axis=0).astype(jnp.float32).reshape(span, HEADS, HD)
        value = jnp.take(values, rows_at, axis=0).astype(jnp.float32).reshape(span, HEADS, HD)
        affinity = jnp.einsum('qhd,khd->hqk', query, key) * factor
        affinity = jnp.where(live[None, None, :], affinity, -1e+30)
        probs = jax.nn.softmax(affinity, axis=-1).astype(jnp.bfloat16)
        context = jnp.einsum('hqk,khd->qhd', probs.astype(jnp.float32), value).astype(jnp.bfloat16).reshape(span, HEADS * HD)
        return (jnp.dot(context, attn_weight, preferred_element_type=jnp.float32), rows_at, live)
    terms, rows_all, live_all = lax.map(one_request, jnp.arange(REQUEST_TOTAL, dtype=jnp.int32))
    target = jnp.where(live_all, rows_all, ROWS).reshape(-1).astype(jnp.int32)
    attention = jnp.zeros((ROWS, TASKS), jnp.float32).at[target].set(terms.reshape(-1, TASKS), mode='drop')
    return jnp.dot(normed, task_weight, preferred_element_type=jnp.float32) + attention
```

```python
import functools
import math

import jax
import jax.numpy as jnp
from jax import lax
from jax.experimental import pallas as pl
from jax.experimental.pallas import tpu as pltpu
from jax.sharding import PartitionSpec as P

HD = 64
ALL = ("wide", "expert", "inner")
VMEM_LIMIT = 60 * 1024 * 1024


def expert_kernel(tasks, x_ref, gate_ref, win_ref, wout_ref, out_ref, acc_ref):
    rows = x_ref.shape[0]
    columns = gate_ref.shape[1]
    experts_all = columns // tasks
    held, _, _ = win_ref.shape
    width = wout_ref.shape[1]
    x = x_ref[...]
    logits = jnp.dot(x, gate_ref[...], preferred_element_type=jnp.float32)
    task = lax.broadcasted_iota(jnp.int32, (rows, columns), 1) // experts_all
    top = jnp.zeros_like(logits)
    for t in range(tasks):
        high = jnp.max(jnp.where(task == t, logits, -jnp.inf), axis=1, keepdims=True)
        top = jnp.where(task == t, high, top)
    powers = jnp.exp(logits - top)
    total = jnp.ones_like(logits)
    for t in range(tasks):
        part = jnp.sum(jnp.where(task == t, powers, 0.0), axis=1, keepdims=True)
        total = jnp.where(task == t, part, total)
    gates = powers / total
    shift = lax.rem(columns - lax.axis_index("expert") * held, columns)
    gates = pltpu.roll(gates, shift, 1)
    together = min(4, held)
    for first in range(0, held, together):
        made = []
        for e in range(first, first + together):
            hidden = jnp.maximum(
                jnp.dot(x, win_ref[e], preferred_element_type=jnp.float32), 0.0
            ).astype(jnp.bfloat16)
            made.append(
                lax.dot_general(
                    hidden,
                    wout_ref[e],
                    (((1,), (1,)), ((), ())),
                    preferred_element_type=jnp.float32,
                )
            )
        for t in range(tasks):
            piece = None
            for j, output in enumerate(made):
                lane = t * experts_all + first + j
                term = gates[:, lane : lane + 1] * output
                piece = term if piece is None else piece + term
            span = slice(t * width, (t + 1) * width)
            if first > 0:
                piece = piece + acc_ref[:, span]
            if first + together < held:
                acc_ref[:, span] = piece
            else:
                out_ref[:, span] = piece.astype(out_ref.dtype)


def run_experts(x, gate_weight, expert_in, expert_out, tasks):
    rows, depth = x.shape
    held, _, units = expert_in.shape
    width = expert_out.shape[1]
    block = min(256, rows)
    return pl.pallas_call(
        functools.partial(expert_kernel, tasks),
        grid=(rows // block,),
        in_specs=[
            pl.BlockSpec((block, depth), lambda i: (i, 0)),
            pl.BlockSpec(gate_weight.shape, lambda i: (0, 0)),
            pl.BlockSpec(expert_in.shape, lambda i: (0, 0, 0), pipeline_mode=pl.Buffered(1)),
            pl.BlockSpec(expert_out.shape, lambda i: (0, 0, 0), pipeline_mode=pl.Buffered(1)),
        ],
        out_specs=pl.BlockSpec((block, tasks * width), lambda i: (i, 0)),
        out_shape=jax.ShapeDtypeStruct((rows, tasks * width), jnp.float32),
        scratch_shapes=[pltpu.VMEM((block, tasks * width), jnp.float32)],
        compiler_params=pltpu.CompilerParams(vmem_limit_bytes=VMEM_LIMIT),
    )(x, gate_weight, expert_in, expert_out)


def attention_kernel(q_ref, k_ref, v_ref, own_ref, all_ref, weight_ref, out_ref):
    same = own_ref[...] == all_ref[...]
    factor = 1.0 / math.sqrt(HD)
    result = None
    for first in range(0, q_ref.shape[1], HD):
        span = slice(first, first + HD)
        affinity = (
            lax.dot_general(
                q_ref[:, span],
                k_ref[:, span],
                (((1,), (1,)), ((), ())),
                preferred_element_type=jnp.float32,
            )
            * factor
        )
        affinity = jnp.where(same, affinity, -1e30)
        highest = jnp.max(affinity, axis=1, keepdims=True)
        powers = jnp.exp(affinity - highest)
        total = jnp.sum(powers, axis=1, keepdims=True)
        context = jnp.dot(
            powers.astype(jnp.bfloat16), v_ref[:, span], preferred_element_type=jnp.float32
        )
        context = (context / total).astype(jnp.bfloat16)
        term = jnp.dot(context, weight_ref[span, :], preferred_element_type=jnp.float32)
        result = term if result is None else result + term
    out_ref[...] = result


def run_attention(q, k, v, own, every, weight):
    rows, width = q.shape
    keys = k.shape[0]
    tasks = weight.shape[1]
    block = min(128, rows)
    return pl.pallas_call(
        attention_kernel,
        grid=(rows // block,),
        in_specs=[
            pl.BlockSpec((block, width), lambda i: (i, 0)),
            pl.BlockSpec((keys, width), lambda i: (0, 0)),
            pl.BlockSpec((keys, width), lambda i: (0, 0)),
            pl.BlockSpec((block, 1), lambda i: (i, 0)),
            pl.BlockSpec((1, keys), lambda i: (0, 0)),
            pl.BlockSpec((width, tasks), lambda i: (0, 0)),
        ],
        out_specs=pl.BlockSpec((block, tasks), lambda i: (i, 0)),
        out_shape=jax.ShapeDtypeStruct((rows, tasks), jnp.float32),
        compiler_params=pltpu.CompilerParams(vmem_limit_bytes=VMEM_LIMIT),
    )(q, k, v, own, every, weight)


def local(
    candidates,
    gate_weight,
    expert_in,
    expert_out,
    norm_gain,
    query_weight,
    key_weight,
    value_weight,
    task_weight,
    attn_weight,
    request_of,
):
    rows = candidates.shape[0]
    tasks = task_weight.shape[1]
    share = rows // (lax.axis_size("expert") * lax.axis_size("inner"))
    spot = lax.axis_index("expert") * lax.axis_size("inner") + lax.axis_index("inner")
    wide = lax.axis_index("wide")
    requests = lax.all_gather(request_of, "wide", axis=0, tiled=True)
    quarter = lax.dynamic_slice_in_dim(candidates, spot * share, share, 0)
    everyone = lax.all_gather(quarter, ALL, axis=0, tiled=True)
    partial_mix = run_experts(everyone, gate_weight, expert_in, expert_out, tasks)
    mixed = lax.psum_scatter(partial_mix, ALL, scatter_dimension=0, tiled=True)
    center = jnp.mean(mixed, axis=1, keepdims=True)
    spread = jnp.mean(jnp.square(mixed - center), axis=1, keepdims=True)
    gain = norm_gain.astype(jnp.float32)
    normed = ((mixed - center) * lax.rsqrt(spread + 1e-05) * gain).astype(jnp.bfloat16)
    normed_all = lax.all_gather(normed, ALL, axis=0, tiled=True)
    own = lax.dynamic_slice_in_dim(normed_all, wide * rows, rows, 0)
    queries = jnp.dot(own, query_weight, preferred_element_type=jnp.float32).astype(jnp.bfloat16)
    keys = jnp.dot(normed_all, key_weight, preferred_element_type=jnp.float32).astype(jnp.bfloat16)
    values = jnp.dot(normed_all, value_weight, preferred_element_type=jnp.float32).astype(
        jnp.bfloat16
    )
    term = run_attention(
        queries, keys, values, request_of[:, None], requests[None, :], attn_weight
    )
    attention = lax.psum(term, ("expert", "inner"))
    return jnp.dot(own, task_weight, preferred_element_type=jnp.float32) + attention


def solution(mesh):
    return jax.shard_map(
        local,
        mesh=mesh,
        in_specs=(
            P(("groups", "wide"), None),
            P(),
            P("expert", None, ("wide", "inner")),
            P("expert", None, ("wide", "inner")),
            P(),
            P(None, ("expert", "inner")),
            P(None, ("expert", "inner")),
            P(None, ("expert", "inner")),
            P(),
            P(("expert", "inner"), None),
            P(("groups", "wide")),
        ),
        out_specs=P(("groups", "wide"), None),
        check_vma=False,
    )
```

```python
import functools
import math

import jax
import jax.numpy as jnp
from jax import lax
from jax.experimental import pallas as pl
from jax.experimental.pallas import tpu as pltpu
from jax.sharding import PartitionSpec as P

HD = 64
ALL = ("wide", "expert", "inner")
VMEM_LIMIT = 60 * 1024 * 1024


MESH = pl.DeviceIdType.MESH


def place():
    return tuple(lax.axis_index(a) for a in ALL), tuple(lax.axis_size(a) for a in ALL)


def turn(start, step, size):
    return lax.rem(start + step, size)


def greet():
    mine, sizes = place()
    barrier = pltpu.get_barrier_semaphore()
    for axis, here, size in zip(ALL, mine, sizes):
        for step in range(1, size):
            pl.semaphore_signal(
                barrier, inc=1, device_id={axis: turn(here, step, size)}, device_id_type=MESH
            )
    pl.semaphore_wait(barrier, sum(sizes) - len(sizes))


def gather_kernel(with_ids, *refs):
    if with_ids:
        own_ref, id_ref, out_ref, ids_ref, recv, send_z, send_x, send_c, local_sem, id_r, id_s = refs
    else:
        own_ref, out_ref, recv, send_z, send_x, send_c, local_sem = refs
    (z, x, c), (nz, nx, nc) = place()
    greet()

    def copy(src, zs, xs, cs, sem, axis, target):
        return pltpu.make_async_remote_copy(
            src_ref=src,
            dst_ref=out_ref.at[zs, cs, xs],
            send_sem=sem,
            recv_sem=recv.at[zs, cs, xs],
            device_id={axis: target},
            device_id_type=MESH,
        )

    def arrived(zs, xs, cs):
        copy(out_ref.at[zs, cs, xs], zs, xs, cs, send_z.at[0], "inner", turn(c, 1, nc)).wait_recv()

    sent = []

    def push(*what):
        item = copy(*what)
        item.start()
        sent.append(item)

    def spread_x(src, k, zs):
        for step in range(1, nx):
            push(src, zs, x, c, send_x.at[k, step - 1], "expert", turn(x, step, nx))

    def spread_c(src, k, j, zs, xs):
        for step in range(1, nc):
            push(src, zs, xs, c, send_c.at[k, j, step - 1], "inner", turn(c, step, nc))

    for step in range(1, nz):
        push(own_ref, z, x, c, send_z.at[step - 1], "wide", turn(z, step, nz))
    spread_x(own_ref, 0, z)
    spread_c(own_ref, 0, 0, z, x)
    keep = pltpu.make_async_copy(own_ref, out_ref.at[z, c, x], local_sem.at[0])
    keep.start()
    if with_ids:
        id_copies = []
        for step in range(1, nz):
            item = pltpu.make_async_remote_copy(
                src_ref=id_ref,
                dst_ref=ids_ref.at[z],
                send_sem=id_s.at[step - 1],
                recv_sem=id_r.at[z],
                device_id={"wide": turn(z, step, nz)},
                device_id_type=MESH,
            )
            item.start()
            id_copies.append(item)
        ids_ref[z] = id_ref[...]

    def pass_x(k):
        zs = turn(z, k, nz)
        for step in range(1, nx):
            xs = turn(x, step, nx)
            arrived(zs, xs, c)
            spread_c(out_ref.at[zs, c, xs], k, step, zs, xs)

    for k in range(1, nz):
        zs = turn(z, k, nz)
        arrived(zs, x, c)
        spread_x(out_ref.at[zs, c, x], k, zs)
        spread_c(out_ref.at[zs, c, x], k, 0, zs, x)
        pass_x(k - 1)
    pass_x(nz - 1)
    for k in range(nz):
        for j in range(nx):
            for step in range(1, nc):
                arrived(turn(z, k, nz), turn(x, j, nx), turn(c, step, nc))
    for item in sent:
        item.wait_send()
    keep.wait()
    if with_ids:
        for step in range(1, nz):
            zs = turn(z, step, nz)
            pltpu.make_async_remote_copy(
                src_ref=id_ref,
                dst_ref=ids_ref.at[zs],
                send_sem=id_s.at[step - 1],
                recv_sem=id_r.at[zs],
                device_id={"wide": zs},
                device_id_type=MESH,
            ).wait_recv()
        for item in id_copies:
            item.wait_send()


def run_gather(own, ids, collective):
    nz, nx, nc = (lax.axis_size(a) for a in ALL)
    dma = pltpu.SemaphoreType.DMA
    with_ids = ids is not None
    shape = jax.ShapeDtypeStruct((nz, nc, nx) + own.shape, own.dtype)
    vmem = pl.BlockSpec(memory_space=pltpu.VMEM)
    anywhere = pl.BlockSpec(memory_space=pl.ANY)
    scratch = [
        dma((nz, nc, nx)),
        dma((max(nz - 1, 1),)),
        dma((nz, max(nx - 1, 1))),
        dma((nz, nx, max(nc - 1, 1))),
        dma((1,)),
    ]
    if with_ids:
        scratch += [dma((nz,)), dma((max(nz - 1, 1),))]
    out = pl.pallas_call(
        functools.partial(gather_kernel, with_ids),
        in_specs=[vmem, vmem] if with_ids else [vmem],
        out_specs=[anywhere, vmem] if with_ids else anywhere,
        out_shape=[shape, jax.ShapeDtypeStruct((nz,) + ids.shape, ids.dtype)] if with_ids else shape,
        scratch_shapes=scratch,
        compiler_params=pltpu.CompilerParams(collective_id=collective, has_side_effects=True),
    )(*([own, ids] if with_ids else [own]))
    depth = own.shape[1]
    if with_ids:
        return out[0].reshape(-1, depth), out[1].reshape(1, -1)
    return out.reshape(-1, depth)


def reduce_kernel(
    part_ref, gain_ref, out_ref, mine, core_in, x_out, x_in, z_out, z_in,
    local_sem, core_s, core_r, x_s, x_r, z_s, z_r,
):
    (z, x, c), (nz, nx, nc) = place()
    f32 = jnp.float32
    greet()
    other = turn(c, 1, nc)
    core, kept = [], []
    for k in range(nz):
        s = turn(z, k + 1, nz)
        item = pltpu.make_async_remote_copy(
            src_ref=part_ref.at[s, other],
            dst_ref=core_in.at[k],
            send_sem=core_s.at[k],
            recv_sem=core_r.at[k],
            device_id={"inner": other},
            device_id_type=MESH,
        )
        item.start()
        core.append(item)
        stay = pltpu.make_async_copy(part_ref.at[s, c], mine.at[k], local_sem.at[k])
        stay.start()
        kept.append(stay)

    def pair(k, xs):
        return mine[k, xs].astype(f32) + core_in[k, xs].astype(f32)

    across, along = [], []

    def finish(k):
        total = pair(k, x)
        for step in range(1, nx):
            across[k][step - 1].wait_recv()
            total = total + x_in[k, step - 1].astype(f32)
        if k == nz - 1:
            return total
        z_out[k] = total.astype(z_out.dtype)
        item = pltpu.make_async_remote_copy(
            src_ref=z_out.at[k],
            dst_ref=z_in.at[k],
            send_sem=z_s.at[k],
            recv_sem=z_r.at[k],
            device_id={"wide": turn(z, k + 1, nz)},
            device_id_type=MESH,
        )
        item.start()
        along.append(item)

    for k in range(nz):
        kept[k].wait()
        core[k].wait_recv()
        items = []
        for step in range(1, nx):
            xs = turn(x, step, nx)
            x_out[k, step - 1] = pair(k, xs).astype(x_out.dtype)
            item = pltpu.make_async_remote_copy(
                src_ref=x_out.at[k, step - 1],
                dst_ref=x_in.at[k, step - 1],
                send_sem=x_s.at[k, step - 1],
                recv_sem=x_r.at[k, step - 1],
                device_id={"expert": xs},
                device_id_type=MESH,
            )
            item.start()
            items.append(item)
        across.append(items)
        if k > 0:
            finish(k - 1)
    total = finish(nz - 1)
    for k in range(nz - 1):
        along[k].wait_recv()
        total = total + z_in[k].astype(f32)
    center = jnp.mean(total, axis=1, keepdims=True)
    spread = jnp.mean(jnp.square(total - center), axis=1, keepdims=True)
    normed = (total - center) * lax.rsqrt(spread + 1e-05) * gain_ref[...].astype(f32)
    out_ref[...] = normed.astype(out_ref.dtype)
    for item in core + along + [i for items in across for i in items]:
        item.wait_send()


def run_reduce(part, gain, share, collective):
    nz, nx, nc = (lax.axis_size(a) for a in ALL)
    width = part.shape[1]
    dma = pltpu.SemaphoreType.DMA
    kind = part.dtype
    part = part.reshape(nz, nc, nx, share, width)
    few = max(nx - 1, 1)
    vmem = pl.BlockSpec(memory_space=pltpu.VMEM)
    return pl.pallas_call(
        reduce_kernel,
        in_specs=[pl.BlockSpec(memory_space=pl.ANY), vmem],
        out_specs=vmem,
        out_shape=jax.ShapeDtypeStruct((share, width), kind),
        scratch_shapes=[
            pltpu.VMEM((nz, nx, share, width), kind),
            pltpu.VMEM((nz, nx, share, width), kind),
            pltpu.VMEM((nz, few, share, width), kind),
            pltpu.VMEM((nz, few, share, width), kind),
            pltpu.VMEM((nz, share, width), kind),
            pltpu.VMEM((nz, share, width), kind),
            dma((nz,)),
            dma((nz,)),
            dma((nz,)),
            dma((nz, few)),
            dma((nz, few)),
            dma((nz,)),
            dma((nz,)),
        ],
        compiler_params=pltpu.CompilerParams(
            collective_id=collective, has_side_effects=True, vmem_limit_bytes=VMEM_LIMIT
        ),
    )(part, gain)


def expert_kernel(tasks, x_ref, gate_ref, win_ref, wout_ref, out_ref, acc_ref):
    rows = x_ref.shape[0]
    columns = gate_ref.shape[1]
    experts_all = columns // tasks
    held, _, _ = win_ref.shape
    width = wout_ref.shape[1]
    x = x_ref[...]
    logits = jnp.dot(x, gate_ref[...], preferred_element_type=jnp.float32)
    task = lax.broadcasted_iota(jnp.int32, (rows, columns), 1) // experts_all
    top = jnp.zeros_like(logits)
    for t in range(tasks):
        high = jnp.max(jnp.where(task == t, logits, -jnp.inf), axis=1, keepdims=True)
        top = jnp.where(task == t, high, top)
    powers = jnp.exp(logits - top)
    total = jnp.ones_like(logits)
    for t in range(tasks):
        part = jnp.sum(jnp.where(task == t, powers, 0.0), axis=1, keepdims=True)
        total = jnp.where(task == t, part, total)
    gates = powers / total
    shift = lax.rem(columns - lax.axis_index("expert") * held, columns)
    gates = pltpu.roll(gates, shift, 1)
    together = min(4, held)
    for first in range(0, held, together):
        made = []
        for e in range(first, first + together):
            hidden = jnp.maximum(
                jnp.dot(x, win_ref[e], preferred_element_type=jnp.float32), 0.0
            ).astype(jnp.bfloat16)
            made.append(
                lax.dot_general(
                    hidden,
                    wout_ref[e],
                    (((1,), (1,)), ((), ())),
                    preferred_element_type=jnp.float32,
                )
            )
        for t in range(tasks):
            piece = None
            for j, output in enumerate(made):
                lane = t * experts_all + first + j
                term = gates[:, lane : lane + 1] * output
                piece = term if piece is None else piece + term
            span = slice(t * width, (t + 1) * width)
            if first > 0:
                piece = piece + acc_ref[:, span]
            if first + together < held:
                acc_ref[:, span] = piece
            else:
                out_ref[:, span] = piece.astype(out_ref.dtype)


def run_experts(x, gate_weight, expert_in, expert_out, tasks):
    rows, depth = x.shape
    held, _, units = expert_in.shape
    width = expert_out.shape[1]
    block = min(256, rows)
    return pl.pallas_call(
        functools.partial(expert_kernel, tasks),
        grid=(rows // block,),
        in_specs=[
            pl.BlockSpec((block, depth), lambda i: (i, 0)),
            pl.BlockSpec(gate_weight.shape, lambda i: (0, 0)),
            pl.BlockSpec(expert_in.shape, lambda i: (0, 0, 0), pipeline_mode=pl.Buffered(1)),
            pl.BlockSpec(expert_out.shape, lambda i: (0, 0, 0), pipeline_mode=pl.Buffered(1)),
        ],
        out_specs=pl.BlockSpec((block, tasks * width), lambda i: (i, 0)),
        out_shape=jax.ShapeDtypeStruct((rows, tasks * width), jnp.bfloat16),
        scratch_shapes=[pltpu.VMEM((block, tasks * width), jnp.float32)],
        compiler_params=pltpu.CompilerParams(vmem_limit_bytes=VMEM_LIMIT),
    )(x, gate_weight, expert_in, expert_out)


def attention_kernel(q_ref, k_ref, v_ref, own_ref, all_ref, weight_ref, out_ref):
    same = own_ref[...] == all_ref[...]
    factor = 1.0 / math.sqrt(HD)
    result = None
    for first in range(0, q_ref.shape[1], HD):
        span = slice(first, first + HD)
        affinity = (
            lax.dot_general(
                q_ref[:, span],
                k_ref[:, span],
                (((1,), (1,)), ((), ())),
                preferred_element_type=jnp.float32,
            )
            * factor
        )
        affinity = jnp.where(same, affinity, -1e30)
        highest = jnp.max(affinity, axis=1, keepdims=True)
        powers = jnp.exp(affinity - highest)
        total = jnp.sum(powers, axis=1, keepdims=True)
        context = jnp.dot(
            powers.astype(jnp.bfloat16), v_ref[:, span], preferred_element_type=jnp.float32
        )
        context = (context / total).astype(jnp.bfloat16)
        term = jnp.dot(context, weight_ref[span, :], preferred_element_type=jnp.float32)
        result = term if result is None else result + term
    out_ref[...] = result


def run_attention(q, k, v, own, every, weight):
    rows, width = q.shape
    keys = k.shape[0]
    tasks = weight.shape[1]
    block = min(128, rows)
    return pl.pallas_call(
        attention_kernel,
        grid=(rows // block,),
        in_specs=[
            pl.BlockSpec((block, width), lambda i: (i, 0)),
            pl.BlockSpec((keys, width), lambda i: (0, 0)),
            pl.BlockSpec((keys, width), lambda i: (0, 0)),
            pl.BlockSpec((block, 1), lambda i: (i, 0)),
            pl.BlockSpec((1, keys), lambda i: (0, 0)),
            pl.BlockSpec((width, tasks), lambda i: (0, 0)),
        ],
        out_specs=pl.BlockSpec((block, tasks), lambda i: (i, 0)),
        out_shape=jax.ShapeDtypeStruct((rows, tasks), jnp.float32),
        compiler_params=pltpu.CompilerParams(vmem_limit_bytes=VMEM_LIMIT),
    )(q, k, v, own, every, weight)


def local(
    candidates,
    gate_weight,
    expert_in,
    expert_out,
    norm_gain,
    query_weight,
    key_weight,
    value_weight,
    task_weight,
    attn_weight,
    request_of,
):
    rows = candidates.shape[0]
    tasks = task_weight.shape[1]
    nx, nc = lax.axis_size("expert"), lax.axis_size("inner")
    share = rows // (nx * nc)
    spot = lax.axis_index("inner") * nx + lax.axis_index("expert")
    wide = lax.axis_index("wide")
    quarter = lax.dynamic_slice_in_dim(candidates, spot * share, share, 0)
    everyone, requests = run_gather(quarter, request_of[None, :], 0)
    partial_mix = run_experts(everyone, gate_weight, expert_in, expert_out, tasks)
    normed = run_reduce(partial_mix, norm_gain[None, :], share, 1)
    normed_all = run_gather(normed, None, 2)
    own = lax.dynamic_slice_in_dim(normed_all, wide * rows, rows, 0)
    queries = jnp.dot(own, query_weight, preferred_element_type=jnp.float32).astype(jnp.bfloat16)
    keys = jnp.dot(normed_all, key_weight, preferred_element_type=jnp.float32).astype(jnp.bfloat16)
    values = jnp.dot(normed_all, value_weight, preferred_element_type=jnp.float32).astype(
        jnp.bfloat16
    )
    term = run_attention(
        queries, keys, values, request_of[:, None], requests, attn_weight
    )
    attention = lax.psum(term, ("expert", "inner"))
    return jnp.dot(own, task_weight, preferred_element_type=jnp.float32) + attention


def solution(mesh):
    return jax.shard_map(
        local,
        mesh=mesh,
        in_specs=(
            P(("groups", "wide"), None),
            P(),
            P("expert", None, ("wide", "inner")),
            P("expert", None, ("wide", "inner")),
            P(),
            P(None, ("expert", "inner")),
            P(None, ("expert", "inner")),
            P(None, ("expert", "inner")),
            P(),
            P(("expert", "inner"), None),
            P(("groups", "wide")),
        ),
        out_specs=P(("groups", "wide"), None),
        check_vma=False,
    )
```

```python
import functools
import math

import jax
import jax.numpy as jnp
from jax import lax
from jax.experimental import pallas as pl
from jax.experimental.pallas import tpu as pltpu
from jax.sharding import PartitionSpec as P

HD = 64
ALL = ("wide", "expert", "inner")
VMEM_LIMIT = 60 * 1024 * 1024


MESH = pl.DeviceIdType.MESH


def place():
    return tuple(lax.axis_index(a) for a in ALL), tuple(lax.axis_size(a) for a in ALL)


def turn(start, step, size):
    return lax.rem(start + step, size)


def greet():
    mine, sizes = place()
    barrier = pltpu.get_barrier_semaphore()
    for axis, here, size in zip(ALL, mine, sizes):
        for step in range(1, size):
            pl.semaphore_signal(
                barrier, inc=1, device_id={axis: turn(here, step, size)}, device_id_type=MESH
            )
    pl.semaphore_wait(barrier, sum(sizes) - len(sizes))


def gather_kernel(with_ids, *refs):
    if with_ids:
        own_ref, id_ref, out_ref, ids_ref, recv, send_z, send_x, send_c, local_sem, id_r, id_s = refs
    else:
        own_ref, out_ref, recv, send_z, send_x, send_c, local_sem = refs
    (z, x, c), (nz, nx, nc) = place()
    greet()

    def copy(src, zs, xs, cs, sem, axis, target):
        return pltpu.make_async_remote_copy(
            src_ref=src,
            dst_ref=out_ref.at[zs, cs, xs],
            send_sem=sem,
            recv_sem=recv.at[zs, cs, xs],
            device_id={axis: target},
            device_id_type=MESH,
        )

    def arrived(zs, xs, cs):
        copy(out_ref.at[zs, cs, xs], zs, xs, cs, send_z.at[0], "inner", turn(c, 1, nc)).wait_recv()

    sent = []

    def push(*what):
        item = copy(*what)
        item.start()
        sent.append(item)

    def spread_x(src, k, zs):
        for step in range(1, nx):
            push(src, zs, x, c, send_x.at[k, step - 1], "expert", turn(x, step, nx))

    def spread_c(src, k, j, zs, xs):
        for step in range(1, nc):
            push(src, zs, xs, c, send_c.at[k, j, step - 1], "inner", turn(c, step, nc))

    for step in range(1, nz):
        push(own_ref, z, x, c, send_z.at[step - 1], "wide", turn(z, step, nz))
    spread_x(own_ref, 0, z)
    spread_c(own_ref, 0, 0, z, x)
    keep = pltpu.make_async_copy(own_ref, out_ref.at[z, c, x], local_sem.at[0])
    keep.start()
    if with_ids:
        id_copies = []
        for step in range(1, nz):
            item = pltpu.make_async_remote_copy(
                src_ref=id_ref,
                dst_ref=ids_ref.at[z],
                send_sem=id_s.at[step - 1],
                recv_sem=id_r.at[z],
                device_id={"wide": turn(z, step, nz)},
                device_id_type=MESH,
            )
            item.start()
            id_copies.append(item)
        ids_ref[z] = id_ref[...]

    def pass_x(k):
        zs = turn(z, k, nz)
        for step in range(1, nx):
            xs = turn(x, step, nx)
            arrived(zs, xs, c)
            spread_c(out_ref.at[zs, c, xs], k, step, zs, xs)

    for k in range(1, nz):
        zs = turn(z, k, nz)
        arrived(zs, x, c)
        spread_x(out_ref.at[zs, c, x], k, zs)
        spread_c(out_ref.at[zs, c, x], k, 0, zs, x)
        pass_x(k - 1)
    pass_x(nz - 1)
    for k in range(nz):
        for j in range(nx):
            for step in range(1, nc):
                arrived(turn(z, k, nz), turn(x, j, nx), turn(c, step, nc))
    for item in sent:
        item.wait_send()
    keep.wait()
    if with_ids:
        for step in range(1, nz):
            zs = turn(z, step, nz)
            pltpu.make_async_remote_copy(
                src_ref=id_ref,
                dst_ref=ids_ref.at[zs],
                send_sem=id_s.at[step - 1],
                recv_sem=id_r.at[zs],
                device_id={"wide": zs},
                device_id_type=MESH,
            ).wait_recv()
        for item in id_copies:
            item.wait_send()


def run_gather(own, ids, collective):
    nz, nx, nc = (lax.axis_size(a) for a in ALL)
    dma = pltpu.SemaphoreType.DMA
    with_ids = ids is not None
    shape = jax.ShapeDtypeStruct((nz, nc, nx) + own.shape, own.dtype)
    vmem = pl.BlockSpec(memory_space=pltpu.VMEM)
    anywhere = pl.BlockSpec(memory_space=pl.ANY)
    scratch = [
        dma((nz, nc, nx)),
        dma((max(nz - 1, 1),)),
        dma((nz, max(nx - 1, 1))),
        dma((nz, nx, max(nc - 1, 1))),
        dma((1,)),
    ]
    if with_ids:
        scratch += [dma((nz,)), dma((max(nz - 1, 1),))]
    out = pl.pallas_call(
        functools.partial(gather_kernel, with_ids),
        in_specs=[vmem, vmem] if with_ids else [vmem],
        out_specs=[anywhere, vmem] if with_ids else anywhere,
        out_shape=[shape, jax.ShapeDtypeStruct((nz,) + ids.shape, ids.dtype)] if with_ids else shape,
        scratch_shapes=scratch,
        compiler_params=pltpu.CompilerParams(collective_id=collective, has_side_effects=True),
    )(*([own, ids] if with_ids else [own]))
    depth = own.shape[1]
    if with_ids:
        return out[0].reshape(-1, depth), out[1].reshape(1, -1)
    return out.reshape(-1, depth)


def reduce_kernel(
    part_ref, gain_ref, out_ref, mine, core_in, x_out, x_in, z_out, z_in,
    local_sem, core_s, core_r, x_s, x_r, z_s, z_r,
):
    (z, x, c), (nz, nx, nc) = place()
    f32 = jnp.float32
    greet()
    other = turn(c, 1, nc)
    core, kept = [], []
    for k in range(nz):
        s = turn(z, k + 1, nz)
        item = pltpu.make_async_remote_copy(
            src_ref=part_ref.at[s, other],
            dst_ref=core_in.at[k],
            send_sem=core_s.at[k],
            recv_sem=core_r.at[k],
            device_id={"inner": other},
            device_id_type=MESH,
        )
        item.start()
        core.append(item)
        stay = pltpu.make_async_copy(part_ref.at[s, c], mine.at[k], local_sem.at[k])
        stay.start()
        kept.append(stay)

    def pair(k, xs):
        return mine[k, xs].astype(f32) + core_in[k, xs].astype(f32)

    across, along = [], []

    def finish(k):
        total = pair(k, x)
        for step in range(1, nx):
            across[k][step - 1].wait_recv()
            total = total + x_in[k, step - 1].astype(f32)
        if k == nz - 1:
            return total
        z_out[k] = total.astype(z_out.dtype)
        item = pltpu.make_async_remote_copy(
            src_ref=z_out.at[k],
            dst_ref=z_in.at[k],
            send_sem=z_s.at[k],
            recv_sem=z_r.at[k],
            device_id={"wide": turn(z, k + 1, nz)},
            device_id_type=MESH,
        )
        item.start()
        along.append(item)

    for k in range(nz):
        kept[k].wait()
        core[k].wait_recv()
        items = []
        for step in range(1, nx):
            xs = turn(x, step, nx)
            x_out[k, step - 1] = pair(k, xs).astype(x_out.dtype)
            item = pltpu.make_async_remote_copy(
                src_ref=x_out.at[k, step - 1],
                dst_ref=x_in.at[k, step - 1],
                send_sem=x_s.at[k, step - 1],
                recv_sem=x_r.at[k, step - 1],
                device_id={"expert": xs},
                device_id_type=MESH,
            )
            item.start()
            items.append(item)
        across.append(items)
        if k > 0:
            finish(k - 1)
    total = finish(nz - 1)
    for k in range(nz - 1):
        along[k].wait_recv()
        total = total + z_in[k].astype(f32)
    center = jnp.mean(total, axis=1, keepdims=True)
    spread = jnp.mean(jnp.square(total - center), axis=1, keepdims=True)
    normed = (total - center) * lax.rsqrt(spread + 1e-05) * gain_ref[...].astype(f32)
    out_ref[...] = normed.astype(out_ref.dtype)
    for item in core + along + [i for items in across for i in items]:
        item.wait_send()


def run_reduce(part, gain, share, collective):
    nz, nx, nc = (lax.axis_size(a) for a in ALL)
    width = part.shape[1]
    dma = pltpu.SemaphoreType.DMA
    kind = part.dtype
    part = part.reshape(nz, nc, nx, share, width)
    few = max(nx - 1, 1)
    vmem = pl.BlockSpec(memory_space=pltpu.VMEM)
    return pl.pallas_call(
        reduce_kernel,
        in_specs=[pl.BlockSpec(memory_space=pl.ANY), vmem],
        out_specs=vmem,
        out_shape=jax.ShapeDtypeStruct((share, width), kind),
        scratch_shapes=[
            pltpu.VMEM((nz, nx, share, width), kind),
            pltpu.VMEM((nz, nx, share, width), kind),
            pltpu.VMEM((nz, few, share, width), kind),
            pltpu.VMEM((nz, few, share, width), kind),
            pltpu.VMEM((nz, share, width), kind),
            pltpu.VMEM((nz, share, width), kind),
            dma((nz,)),
            dma((nz,)),
            dma((nz,)),
            dma((nz, few)),
            dma((nz, few)),
            dma((nz,)),
            dma((nz,)),
        ],
        compiler_params=pltpu.CompilerParams(
            collective_id=collective, has_side_effects=True, vmem_limit_bytes=VMEM_LIMIT
        ),
    )(part, gain)


def expert_kernel(tasks, x_ref, gate_ref, win_ref, wout_ref, out_ref, acc_ref):
    rows = x_ref.shape[0]
    columns = gate_ref.shape[1]
    experts_all = columns // tasks
    held, _, _ = win_ref.shape
    width = wout_ref.shape[1]
    x = x_ref[...]
    logits = jnp.dot(x, gate_ref[...], preferred_element_type=jnp.float32)
    task = lax.broadcasted_iota(jnp.int32, (rows, columns), 1) // experts_all
    top = jnp.zeros_like(logits)
    for t in range(tasks):
        high = jnp.max(jnp.where(task == t, logits, -jnp.inf), axis=1, keepdims=True)
        top = jnp.where(task == t, high, top)
    powers = jnp.exp(logits - top)
    total = jnp.ones_like(logits)
    for t in range(tasks):
        part = jnp.sum(jnp.where(task == t, powers, 0.0), axis=1, keepdims=True)
        total = jnp.where(task == t, part, total)
    gates = powers / total
    shift = lax.rem(columns - lax.axis_index("expert") * held, columns)
    gates = pltpu.roll(gates, shift, 1)
    together = min(4, held)
    for first in range(0, held, together):
        made = []
        for e in range(first, first + together):
            hidden = jnp.maximum(
                jnp.dot(x, win_ref[e], preferred_element_type=jnp.float32), 0.0
            ).astype(jnp.bfloat16)
            made.append(
                lax.dot_general(
                    hidden,
                    wout_ref[e],
                    (((1,), (1,)), ((), ())),
                    preferred_element_type=jnp.float32,
                )
            )
        for t in range(tasks):
            piece = None
            for j, output in enumerate(made):
                lane = t * experts_all + first + j
                term = gates[:, lane : lane + 1] * output
                piece = term if piece is None else piece + term
            span = slice(t * width, (t + 1) * width)
            if first > 0:
                piece = piece + acc_ref[:, span]
            if first + together < held:
                acc_ref[:, span] = piece
            else:
                out_ref[:, span] = piece.astype(out_ref.dtype)


def run_experts(x, gate_weight, expert_in, expert_out, tasks):
    rows, depth = x.shape
    held, _, units = expert_in.shape
    width = expert_out.shape[1]
    block = min(512, rows)
    return pl.pallas_call(
        functools.partial(expert_kernel, tasks),
        grid=(rows // block,),
        in_specs=[
            pl.BlockSpec((block, depth), lambda i: (i, 0)),
            pl.BlockSpec(gate_weight.shape, lambda i: (0, 0)),
            pl.BlockSpec(expert_in.shape, lambda i: (0, 0, 0), pipeline_mode=pl.Buffered(1)),
            pl.BlockSpec(expert_out.shape, lambda i: (0, 0, 0), pipeline_mode=pl.Buffered(1)),
        ],
        out_specs=pl.BlockSpec((block, tasks * width), lambda i: (i, 0)),
        out_shape=jax.ShapeDtypeStruct((rows, tasks * width), jnp.bfloat16),
        scratch_shapes=[pltpu.VMEM((block, tasks * width), jnp.float32)],
        compiler_params=pltpu.CompilerParams(vmem_limit_bytes=VMEM_LIMIT),
    )(x, gate_weight, expert_in, expert_out)


def attention_kernel(q_ref, k_ref, v_ref, own_ref, all_ref, weight_ref, out_ref):
    same = own_ref[...] == all_ref[...]
    factor = 1.0 / math.sqrt(HD)
    result = None
    for first in range(0, q_ref.shape[1], HD):
        span = slice(first, first + HD)
        affinity = (
            lax.dot_general(
                q_ref[:, span],
                k_ref[:, span],
                (((1,), (1,)), ((), ())),
                preferred_element_type=jnp.float32,
            )
            * factor
        )
        affinity = jnp.where(same, affinity, -1e30)
        highest = jnp.max(affinity, axis=1, keepdims=True)
        powers = jnp.exp(affinity - highest)
        total = jnp.sum(powers, axis=1, keepdims=True)
        context = jnp.dot(
            powers.astype(jnp.bfloat16), v_ref[:, span], preferred_element_type=jnp.float32
        )
        context = (context / total).astype(jnp.bfloat16)
        term = jnp.dot(context, weight_ref[span, :], preferred_element_type=jnp.float32)
        result = term if result is None else result + term
    out_ref[...] = result


def run_attention(q, k, v, own, every, weight):
    rows, width = q.shape
    keys = k.shape[0]
    tasks = weight.shape[1]
    block = min(128, rows)
    return pl.pallas_call(
        attention_kernel,
        grid=(rows // block,),
        in_specs=[
            pl.BlockSpec((block, width), lambda i: (i, 0)),
            pl.BlockSpec((keys, width), lambda i: (0, 0)),
            pl.BlockSpec((keys, width), lambda i: (0, 0)),
            pl.BlockSpec((block, 1), lambda i: (i, 0)),
            pl.BlockSpec((1, keys), lambda i: (0, 0)),
            pl.BlockSpec((width, tasks), lambda i: (0, 0)),
        ],
        out_specs=pl.BlockSpec((block, tasks), lambda i: (i, 0)),
        out_shape=jax.ShapeDtypeStruct((rows, tasks), jnp.float32),
        compiler_params=pltpu.CompilerParams(vmem_limit_bytes=VMEM_LIMIT),
    )(q, k, v, own, every, weight)


def local(
    candidates,
    gate_weight,
    expert_in,
    expert_out,
    norm_gain,
    query_weight,
    key_weight,
    value_weight,
    task_weight,
    attn_weight,
    request_of,
):
    rows = candidates.shape[0]
    tasks = task_weight.shape[1]
    nx, nc = lax.axis_size("expert"), lax.axis_size("inner")
    share = rows // (nx * nc)
    spot = lax.axis_index("inner") * nx + lax.axis_index("expert")
    wide = lax.axis_index("wide")
    quarter = lax.dynamic_slice_in_dim(candidates, spot * share, share, 0)
    everyone, requests = run_gather(quarter, request_of[None, :], 0)
    partial_mix = run_experts(everyone, gate_weight, expert_in, expert_out, tasks)
    normed = run_reduce(partial_mix, norm_gain[None, :], share, 1)
    normed_all = run_gather(normed, None, 2)
    own = lax.dynamic_slice_in_dim(normed_all, wide * rows, rows, 0)
    queries = jnp.dot(own, query_weight, preferred_element_type=jnp.float32).astype(jnp.bfloat16)
    keys = jnp.dot(normed_all, key_weight, preferred_element_type=jnp.float32).astype(jnp.bfloat16)
    values = jnp.dot(normed_all, value_weight, preferred_element_type=jnp.float32).astype(
        jnp.bfloat16
    )
    term = run_attention(
        queries, keys, values, request_of[:, None], requests, attn_weight
    )
    attention = lax.psum(term.T, ("expert", "inner")).T
    return jnp.dot(own, task_weight, preferred_element_type=jnp.float32) + attention


def solution(mesh):
    return jax.shard_map(
        local,
        mesh=mesh,
        in_specs=(
            P(("groups", "wide"), None),
            P(),
            P("expert", None, ("wide", "inner")),
            P("expert", None, ("wide", "inner")),
            P(),
            P(None, ("expert", "inner")),
            P(None, ("expert", "inner")),
            P(None, ("expert", "inner")),
            P(),
            P(("expert", "inner"), None),
            P(("groups", "wide")),
        ),
        out_specs=P(("groups", "wide"), None),
        check_vma=False,
    )
```
